1024 devices in a mesh: replica: 64 (over y_lo, z), shard: 16 (over x, y_hi, core).
Axes of the slice: x: 4, y: 4 (y_hi: 2, y_lo: 2; y = y_hi * 2 + y_lo), z: 32, core: 2. Of those that a mesh axis runs over, the one named last changes fastest.
Arguments:
- features: bfloat16 [16384, 4096], P('replica', 'shard'), may hold values from -6 to 6
- weight: bfloat16 [128, 1024, 128], P('shard'), may hold values from -0.1875 to 0.1875
- rows_index: int32 [128, 8], replicated, may hold values from 0 to 31, as said below
- cotangent: bfloat16 [16384, 16384], P('replica', 'shard'), may hold values from -6 to 6
Outputs:
- activated: bfloat16 [16384, 16384], P('replica', 'shard')
- input_grad: bfloat16 [16384, 4096], P('replica', 'shard')
- weight_grad: float32 [128, 1024, 128], P('shard', 'replica')
The draws below stay inside these ranges and needn't reach their ends.
Inputs may be any that keep to these rules, and one draw needn't show every extreme that they name: `rows_index`: each block column lists 8 different block rows.
All inputs are finite; a program needn't handle non-finite values.
Results may differ from the reference program's by a relative error of at most 0.02.
Values may be sent and summed in bfloat16 or wider, within the bound.
A program may use at most 64 MiB of HBM per device.

```python
import math
import jax
import jax.numpy as jnp
from jax import lax

D = 4096
FF = 16384
BLK = 128
K = 8
NBR = 32
NCOL = 128
TOKENS = 16384
N_SHARD = 16


def draw_rows_index(key, part):
    keys = jax.random.split(jax.random.fold_in(key, 7), NCOL)

    def pick_rows(one_key):
        return jax.random.permutation(one_key, jnp.arange(NBR, dtype=jnp.int32))[:K]
    return jax.vmap(pick_rows)(keys).astype(jnp.int32)


def steps_of(stream_key, shape, cuts, least, top_value):
    level = 1.0
    for position, parts in cuts:
        heights = jax.random.uniform(jax.random.fold_in(jax.random.fold_in(stream_key, 6), position), (parts,), jnp.float32, least / len(cuts), top_value / len(cuts))
        level = level * jnp.repeat(jnp.exp(heights), shape[position] // parts).reshape((-1,) + (1,) * (len(shape) - 1 - position))
    return level


def normal_values(rng, shape, scale, limit, pieces=(), kind=jnp.bfloat16):
    values = jax.random.normal(rng, shape, jnp.float32) * scale
    if len(pieces) > 0:
        values = steps_of(rng, shape, pieces, -0.22, 0.18) * values
    return jnp.clip(values, min=-limit, max=limit).astype(kind)


def setup_inputs(seed: int = 0) -> dict:
    splits = jax.random.split(jax.random.key(seed), 5)
    return {
        "features": normal_values(splits[0], (TOKENS, D), 1.0, 6.0, ((0, 64), (1, 16))),
        "weight": normal_values(splits[1], (NCOL, K * BLK, BLK), (K * BLK) ** -0.5, 0.1875, ((0, 16),)),
        "rows_index": draw_rows_index(jax.random.fold_in(splits[4], 71), 0),
        "cotangent": normal_values(splits[3], (TOKENS, FF), 1.0, 6.0, ((0, 64), (1, 16))),
    }


def reference(features, weight, rows_index, cotangent):
    groups = NCOL // N_SHARD
    blocks = features.reshape(TOKENS, NBR, BLK).astype(jnp.float32)
    block_weight_tiles = weight.reshape(NCOL, K, BLK, BLK).astype(jnp.float32)
    cot_blocks = cotangent.reshape(TOKENS, NCOL, BLK)
    positions = jnp.arange(NBR, dtype=jnp.int32)

    def per_group(carry, group):
        columns = group * groups + jnp.arange(groups, dtype=jnp.int32)
        chosen = rows_index[columns]
        resident_weights = block_weight_tiles[columns]
        selected_rows = blocks[:, chosen]
        preactivation = jnp.einsum('defv,efvp->dep', selected_rows, resident_weights)
        sig = jax.nn.sigmoid(preactivation)
        activated = (preactivation * sig).astype(jnp.bfloat16)
        slope = cot_blocks[:, columns].astype(jnp.float32) * sig * (1.0 + preactivation * (1.0 - sig))
        output_difference = lax.optimization_barrier(slope.astype(jnp.bfloat16)).astype(jnp.float32)
        gradient_list = jnp.einsum('qlpf,qlx->lpfx', selected_rows, output_difference)
        backward_result = jnp.einsum('iov,omgv->iomg', output_difference, resident_weights)
        onehot = (chosen[:, :, None] == positions[None, None, :]).astype(jnp.float32)
        partial_value = jnp.einsum('tckr,ckb->tbr', backward_result, onehot)
        partial_value = lax.optimization_barrier(partial_value.astype(jnp.bfloat16)).astype(jnp.float32)
        return (carry + partial_value, (activated, gradient_list))
    start = jnp.zeros((TOKENS, NBR, BLK), jnp.float32)
    summed, (acts, gradient_list) = lax.scan(per_group, start, jnp.arange(N_SHARD, dtype=jnp.int32))
    activated = jnp.transpose(acts, (1, 0, 2, 3)).reshape(TOKENS, FF)
    input_grad = summed.reshape(TOKENS, D).astype(jnp.bfloat16)
    weight_grad = gradient_list.reshape(NCOL, K * BLK, BLK) * (1.0 / math.sqrt(TOKENS))
    return (activated, input_grad, weight_grad)
```

```python
import math

import jax
import jax.numpy as jnp
from jax import lax
from jax.experimental import pallas as pl
from jax.experimental.pallas import tpu as pltpu
from jax.sharding import PartitionSpec as P

MESH = pl.DeviceIdType.MESH
F32, BF16 = jnp.float32, jnp.bfloat16
NX, NZ = 4, 32
NG = 2


def dot_nn(a, b):
    return lax.dot_general(a, b, (((1,), (0,)), ((), ())), preferred_element_type=F32)


def dot_nt(a, b):
    return lax.dot_general(a, b, (((1,), (1,)), ((), ())), preferred_element_type=F32)


def kernel(
    rows, feat, w_hbm, cot_hbm,
    act_out, ig_out, wg_out,
    xt, wz, wt, wd, cot, cott, dt, xs, act, own,
    zsend, zrecv, ysend, yrecv, csend, crecv, gsend, grecv, gown,
    local_sem, act_sem, ag_s, ag_r, z_s, z_r, y_s, y_r, c_s, c_r, g_s, g_r,
):
    tokens = feat.shape[0]
    ncol = wt.shape[0]
    per_group = ncol // NG
    r = lax.axis_index("replica")
    s = lax.axis_index("shard")
    ylo, z = r // NZ, r % NZ
    x, yh, core = s // 4, (s // 2) % 2, s % 2

    def shard_at(dx, dy, dc):
        return ((x + dx) % NX) * 4 + ((yh + dy) % 2) * 2 + (core + dc) % 2

    def dev_shard(dx, dy, dc):
        return {"replica": r, "shard": shard_at(dx, dy, dc)}

    def dev_z(step):
        return {"replica": ylo * NZ + (z + step + NZ) % NZ, "shard": s}

    dev_y = {"replica": (1 - ylo) * NZ + z, "shard": s}
    offsets = [(dx, dy) for dy in (0, 1) for dx in (0, 1, 3, 2)]

    w_copy = pltpu.make_async_copy(w_hbm, wz.at[pl.ds(0, w_hbm.shape[0])], local_sem.at[0])
    w_copy.start()
    cot_copy = pltpu.make_async_copy(cot_hbm, cot, local_sem.at[1])
    cot_copy.start()

    barrier = pltpu.get_barrier_semaphore()
    peers = [dev_shard(dx, dy, 0) for dx, dy in offsets[1:]] + [dev_shard(0, 0, 1), dev_z(1), dev_z(-1), dev_y]
    for peer in peers:
        pl.semaphore_signal(barrier, inc=1, device_id=peer, device_id_type=MESH)

    mine = feat[...].T.reshape(2, feat.shape[1] // 2, tokens)
    xt[pl.ds(2 * s, 2)] = mine
    pl.semaphore_wait(barrier, len(peers))

    sends = []

    def remote(src, dst, send_sem, recv_sem, device):
        return pltpu.make_async_remote_copy(
            src_ref=src, dst_ref=dst, send_sem=send_sem, recv_sem=recv_sem,
            device_id=device, device_id_type=MESH,
        )

    def push(*args):
        copy = remote(*args)
        copy.start()
        sends.append(copy)

    right, left = dev_shard(1, 0, 0), dev_shard(3, 0, 0)
    across, sibling = dev_shard(0, 1, 0), dev_shard(0, 0, 1)

    def half(dx, dy, h):
        return xt.at[2 * shard_at(dx, dy, 0) + h]

    def block(dx, dy, dc=0):
        return xt.at[pl.ds(2 * shard_at(dx, dy, dc), 2)]

    def gather_send(m, ref, device):
        push(ref, ref, ag_s.at[m], ag_r.at[m], device)

    def gather_wait(m, ref):
        remote(ref, ref, ag_s.at[m], ag_r.at[m], sibling).wait_recv()

    gather_send(0, half(0, 0, 0), right)
    gather_send(3, half(0, 0, 1), left)
    gather_send(4, half(0, 0, 0), across)
    gather_send(5, half(0, 0, 1), across)
    gather_send(1, half(0, 0, 1), right)
    gather_send(2, half(0, 0, 0), left)
    gather_send(14, block(0, 0), sibling)

    def transpose_cot():
        cot_copy.wait()
        for c in range(ncol):
            cott[c] = cot[:, c * 128 : (c + 1) * 128].T

    def transpose_w(c):
        wt[c] = wz[pl.ds(8 * c, 8)].reshape(8 * 128, 128).T

    def dense_w(c):
        listed = [rows[k, s * ncol + c] for k in range(8)]

        def body(b, carry):
            index = 8 * ncol
            for k in range(8):
                index = jnp.where(listed[k] == b, 8 * c + k, index)
            wd[b, :, c * 128 : (c + 1) * 128] = wz[index]
            return carry

        lax.fori_loop(0, 32, body, 0)

    w_copy.wait()
    wz[8 * ncol] = jnp.zeros((128, 128), BF16)
    transpose_w(0)
    transpose_w(1)

    gather_wait(0, half(3, 0, 0))
    gather_send(6, half(3, 0, 0), right)
    gather_wait(3, half(1, 0, 1))
    gather_send(7, half(1, 0, 1), left)
    transpose_w(2)
    transpose_w(3)
    gather_wait(4, half(0, 1, 0))
    gather_send(8, half(0, 1, 0), right)
    gather_send(10, half(0, 1, 0), left)
    gather_wait(5, half(0, 1, 1))
    gather_send(11, half(0, 1, 1), left)
    gather_send(9, half(0, 1, 1), right)
    gather_send(17, block(0, 1), sibling)
    gather_wait(1, half(3, 0, 1))
    gather_send(15, block(3, 0), sibling)
    gather_wait(2, half(1, 0, 0))
    gather_send(16, block(1, 0), sibling)
    for c in range(4, ncol):
        transpose_w(c)
    gather_wait(6, half(2, 0, 0))
    gather_wait(7, half(2, 0, 1))
    gather_send(18, block(2, 0), sibling)
    transpose_cot()
    gather_wait(8, half(3, 1, 0))
    gather_send(12, half(3, 1, 0), right)
    gather_wait(11, half(1, 1, 1))
    gather_send(13, half(1, 1, 1), left)
    gather_wait(9, half(3, 1, 1))
    gather_send(19, block(3, 1), sibling)
    gather_wait(10, half(1, 1, 0))
    gather_send(20, block(1, 1), sibling)
    dense_w(0)
    dense_w(1)
    gather_wait(12, half(2, 1, 0))
    gather_wait(13, half(2, 1, 1))
    gather_send(21, block(2, 1), sibling)
    for m, (dx, dy) in zip(range(14, 22), ((0, 0), (3, 0), (1, 0), (0, 1), (2, 0), (3, 1), (1, 1), (2, 1))):
        gather_wait(m, block(dx, dy, 1))

    act_copies = []

    def column(c):
        for k in range(8):
            xs[c % 2, k * 128 : (k + 1) * 128, :] = xt[rows[k, s * ncol + c]]
        pre = dot_nn(wt[c], xs[c % 2])
        sig = jax.nn.sigmoid(pre)
        act[:, c * 128 : (c + 1) * 128] = (pre * sig).T.astype(BF16)
        slope = cott[c].astype(F32) * sig * (1.0 + pre * (1.0 - sig))
        dt[c * 128 : (c + 1) * 128, :] = slope.astype(BF16)
        grad = dot_nt(xs[c % 2], dt[c * 128 : (c + 1) * 128, :])
        own[c] = grad.reshape(2, NZ, 16, 128)

    top = (NZ // 2, NZ // 2 - 1)
    sign = (1, -1)

    def own_part(g, owner):
        return own[per_group * g : per_group * (g + 1), :, owner]

    def z_wait(g, d, n):
        remote(zsend.at[g, d, n], zrecv.at[g, d, n], z_s.at[g, d, n], z_r.at[g, d, n], sibling).wait_recv()

    def ring(g, j):
        for d in (0, 1):
            n = top[d] - j
            if n < 1:
                continue
            total = own_part(g, (z + sign[d] * n + NZ) % NZ)
            if j > 0:
                z_wait(g, d, n)
                total = total + zrecv[g, d, n].astype(F32)
            zsend[g, d, n] = total.astype(BF16)
            push(zsend.at[g, d, n], zrecv.at[g, d, n - 1], z_s.at[g, d, n], z_r.at[g, d, n - 1], dev_z(sign[d]))

    def ring_end(g):
        z_wait(g, 1, 0)
        z_wait(g, 0, 0)
        low = per_group * g
        other = own[low : low + per_group, 1 - ylo, z]
        for d in (0, 1):
            other = other + zrecv[g, d, 0, :, 1 - ylo].astype(F32)
        ysend[g] = other.astype(BF16)
        push(ysend.at[g], yrecv.at[g], y_s.at[g], y_r.at[g], dev_y)

    def finish(g, scale):
        low = per_group * g
        total = own[low : low + per_group, ylo, z]
        for d in (0, 1):
            total = total + zrecv[g, d, 0, :, ylo].astype(F32)
        remote(ysend.at[g], yrecv.at[g], y_s.at[g], y_r.at[g], dev_y).wait_recv()
        wg_out[low : low + per_group] = (total + yrecv[g].astype(F32)) * scale

    def partial(dx, dy, dc):
        weights = wd[pl.ds(2 * shard_at(dx, dy, dc), 2)].reshape(256, ncol * 128)
        return dot_nn(weights, dt[...])

    def sibling_task(p):
        dx, dy = offsets[p]
        csend[p] = partial(dx, dy, 1).astype(BF16)
        push(csend.at[p], crecv.at[p], c_s.at[p], c_r.at[p], sibling)

    def chip_task(p):
        dx, dy = offsets[p]
        total = partial(dx, dy, 0)
        remote(csend.at[p], crecv.at[p], c_s.at[p], c_r.at[p], sibling).wait_recv()
        total = total + crecv[p].astype(F32)
        if p == 0:
            gown[...] = total
            return
        gsend[p - 1] = total.astype(BF16)
        push(gsend.at[p - 1], grecv.at[p - 1], g_s.at[p - 1], g_r.at[p - 1], dev_shard(dx, dy, 0))

    def gather_grad():
        total = gown[...]
        for p in range(1, 8):
            remote(gsend.at[p - 1], grecv.at[p - 1], g_s.at[p - 1], g_r.at[p - 1], sibling).wait_recv()
            total = total + grecv[p - 1].astype(F32)
        ig_out[...] = total.T.astype(BF16)

    steps = NZ // 2
    tasks = [lambda p=p: sibling_task(p) for p in (7, 6, 5, 4, 3, 2, 1, 0)]
    tasks += [lambda p=p: chip_task(p) for p in (7, 6, 5, 4, 3, 2, 1, 0)]
    tasks = [lambda c=c: dense_w(c) for c in range(2, ncol)] + tasks
    todo = [0] * NG
    for c in range(ncol):
        column(c)
        for g in range(NG):
            if (c + 1) >= per_group * (g + 1) and todo[g] < steps:
                ring(g, todo[g])
                todo[g] += 1
    act_copy = pltpu.make_async_copy(act, act_out, act_sem)
    act_copy.start()
    while min(todo) < steps:
        for g in range(NG):
            if todo[g] < steps:
                if tasks:
                    tasks.pop(0)()
                ring(g, todo[g])
                todo[g] += 1
    while tasks:
        tasks.pop(0)()
    for g in range(NG):
        ring_end(g)
    gather_grad()
    scale = 1.0 / math.sqrt(tokens * lax.axis_size("replica"))
    for g in range(NG):
        finish(g, scale)
    for copy in sends:
        copy.wait_send()
    act_copy.wait()


def local(features, weight, rows_index, cotangent):
    tokens, width = features.shape
    columns, depth, side = weight.shape
    blocks = columns * depth // side
    per_group = columns // NG
    dma = pltpu.SemaphoreType.DMA
    vmem = pl.BlockSpec(memory_space=pltpu.VMEM)
    anywhere = pl.BlockSpec(memory_space=pl.ANY)
    return pl.pallas_call(
        kernel,
        out_shape=(
            jax.ShapeDtypeStruct((tokens, columns * side), BF16),
            jax.ShapeDtypeStruct((tokens, width), BF16),
            jax.ShapeDtypeStruct((columns, 16, side), F32),
        ),
        in_specs=[pl.BlockSpec(memory_space=pltpu.SMEM), vmem, anywhere, anywhere],
        out_specs=(anywhere, vmem, vmem),
        scratch_shapes=[
            pltpu.VMEM((32, side, tokens), BF16),
            pltpu.VMEM((blocks + 1, side, side), BF16),
            pltpu.VMEM((columns, side, depth), BF16),
            pltpu.VMEM((32, side, columns * side), BF16),
            pltpu.VMEM((tokens, columns * side), BF16),
            pltpu.VMEM((columns, side, tokens), BF16),
            pltpu.VMEM((columns * side, tokens), BF16),
            pltpu.VMEM((2, depth, tokens), BF16),
            pltpu.VMEM((tokens, columns * side), BF16),
            pltpu.VMEM((columns, 2, NZ, 16, side), F32),
            pltpu.VMEM((NG, 2, NZ // 2 + 1, per_group, 2, 16, side), BF16),
            pltpu.VMEM((NG, 2, NZ // 2 + 1, per_group, 2, 16, side), BF16),
            pltpu.VMEM((NG, per_group, 16, side), BF16),
            pltpu.VMEM((NG, per_group, 16, side), BF16),
            pltpu.VMEM((8, 2 * side, tokens), BF16),
            pltpu.VMEM((8, 2 * side, tokens), BF16),
            pltpu.VMEM((7, 2 * side, tokens), BF16),
            pltpu.VMEM((7, 2 * side, tokens), BF16),
            pltpu.VMEM((2 * side, tokens), F32),
            dma((2,)), dma,
            dma((22,)), dma((22,)),
            dma((NG, 2, NZ // 2 + 1)), dma((NG, 2, NZ // 2 + 1)),
            dma((NG,)), dma((NG,)),
            dma((8,)), dma((8,)),
            dma((7,)), dma((7,)),
        ],
        compiler_params=pltpu.CompilerParams(
            collective_id=0, has_side_effects=True, vmem_limit_bytes=56 * 2**20
        ),
        name="fused",
    )(rows_index.T, features, weight.reshape(blocks, side, side), cotangent)


def solution(mesh):
    placed = (P("replica", "shard"), P("shard", None, None), P(), P("replica", "shard"))
    return jax.shard_map(
        local,
        mesh=mesh,
        in_specs=placed,
        out_specs=(P("replica", "shard"), P("replica", "shard"), P("shard", "replica", None)),
        check_vma=False,
    )
```

```python
import math

import jax
import jax.numpy as jnp
from jax import lax
from jax.experimental import pallas as pl
from jax.experimental.pallas import tpu as pltpu
from jax.sharding import PartitionSpec as P

MESH = pl.DeviceIdType.MESH
F32, BF16 = jnp.float32, jnp.bfloat16
NX, NZ = 4, 32


def dot_nn(a, b):
    return lax.dot_general(a, b, (((1,), (0,)), ((), ())), preferred_element_type=F32)


def dot_nt(a, b):
    return lax.dot_general(a, b, (((1,), (1,)), ((), ())), preferred_element_type=F32)


NB = 4
PARENT = (-1, 0, 1, 2, 0, 4, 5, 6, 4, 8, 9, 10, 8, 12, 12, 14)


def hop(e):
    return e - PARENT[e]


def children(e, top):
    return [child for child in range(top) if PARENT[child] == e]


def kernel(
    rows, feat, w_hbm, cot_hbm,
    act_out, ig_out, wg_out,
    xt, wz, wt, wd, cot, cott, dt, xs, act, own,
    asend, arecv, bsend, brecv, ysend, yrecv, fsend, frecv, csend, crecv, gsend, grecv, gown,
    local_sem, act_sem, ag_s, ag_r, a_s, a_r, b_s, b_r, y_s, y_r, f_s, f_r, c_s, c_r, g_s, g_r,
):
    tokens = feat.shape[0]
    ncol = wt.shape[0]
    r = lax.axis_index("replica")
    s = lax.axis_index("shard")
    ylo, z = r // NZ, r % NZ
    x, yh, core = s // 4, (s // 2) % 2, s % 2
    top = (NZ // 2, NZ // 2 - 1)
    sign = (1, -1)

    def shard_at(dx, dy, dc):
        return ((x + dx) % NX) * 4 + ((yh + dy) % 2) * 2 + (core + dc) % 2

    def dev_shard(dx, dy, dc):
        return {"replica": r, "shard": shard_at(dx, dy, dc)}

    def dev_z(step):
        return {"replica": ylo * NZ + (z + step + NZ) % NZ, "shard": s}

    dev_y = {"replica": (1 - ylo) * NZ + z, "shard": s}
    sibling = dev_shard(0, 0, 1)
    others = ((2, 1), (1, 1), (3, 1), (2, 0), (0, 1), (1, 0), (3, 0))

    w_copy = pltpu.make_async_copy(w_hbm, wz.at[pl.ds(0, w_hbm.shape[0])], local_sem.at[0])
    w_copy.start()
    cot_copy = pltpu.make_async_copy(cot_hbm, cot, local_sem.at[1])
    cot_copy.start()

    barrier = pltpu.get_barrier_semaphore()
    peers = [dev_shard(dx, dy, 0) for dx, dy in others] + [sibling, dev_y]
    peers += [dev_z(d * h) for h in sorted({hop(e) for e in range(len(PARENT))}) for d in sign]
    for peer in peers:
        pl.semaphore_signal(barrier, inc=1, device_id=peer, device_id_type=MESH)

    mine = feat[...].T.reshape(2, feat.shape[1] // 2, tokens)
    xt[pl.ds(2 * s, 2)] = mine
    pl.semaphore_wait(barrier, len(peers))

    sends = []

    def remote(src, dst, send_sem, recv_sem, device):
        return pltpu.make_async_remote_copy(
            src_ref=src, dst_ref=dst, send_sem=send_sem, recv_sem=recv_sem,
            device_id=device, device_id_type=MESH,
        )

    def push(*args):
        copy = remote(*args)
        copy.start()
        sends.append(copy)

    right, left = dev_shard(1, 0, 0), dev_shard(3, 0, 0)
    across = dev_shard(0, 1, 0)

    def half(dx, dy, h):
        return xt.at[2 * shard_at(dx, dy, 0) + h]

    def block(dx, dy, dc=0):
        return xt.at[pl.ds(2 * shard_at(dx, dy, dc), 2)]

    def gather_send(m, ref, device):
        push(ref, ref, ag_s.at[m], ag_r.at[m], device)

    def gather_wait(m, ref):
        remote(ref, ref, ag_s.at[m], ag_r.at[m], sibling).wait_recv()

    gather_send(0, half(0, 0, 0), right)
    gather_send(3, half(0, 0, 1), left)
    gather_send(4, half(0, 0, 0), across)
    gather_send(5, half(0, 0, 1), across)
    gather_send(1, half(0, 0, 1), right)
    gather_send(2, half(0, 0, 0), left)
    gather_send(14, block(0, 0), sibling)

    def transpose_cot():
        cot_copy.wait()
        for c in range(ncol):
            cott[c] = cot[:, c * 128 : (c + 1) * 128].T

    def transpose_w(c):
        for part, first in ((0, ylo), (1, 1 - ylo)):
            four = wz[pl.ds(8 * c + 4 * first, 4)].reshape(4 * 128, 128)
            wt[c, :, part * 512 : (part + 1) * 512] = four.T

    def dense_w(c):
        listed = [rows[k, s * ncol + c] for k in range(8)]

        def body(b, carry):
            index = 8 * ncol
            for k in range(8):
                index = jnp.where(listed[k] == b, 8 * c + k, index)
            wd[b, :, c * 128 : (c + 1) * 128] = wz[index]
            return carry

        lax.fori_loop(0, 32, body, 0)

    w_copy.wait()
    wz[8 * ncol] = jnp.zeros((128, 128), BF16)
    transpose_w(0)
    transpose_w(1)

    gather_wait(0, half(3, 0, 0))
    gather_send(6, half(3, 0, 0), right)
    gather_wait(3, half(1, 0, 1))
    gather_send(7, half(1, 0, 1), left)
    transpose_w(2)
    transpose_w(3)
    gather_wait(4, half(0, 1, 0))
    gather_send(8, half(0, 1, 0), right)
    gather_send(10, half(0, 1, 0), left)
    gather_wait(5, half(0, 1, 1))
    gather_send(11, half(0, 1, 1), left)
    gather_send(9, half(0, 1, 1), right)
    gather_send(17, block(0, 1), sibling)
    gather_wait(1, half(3, 0, 1))
    gather_send(15, block(3, 0), sibling)
    gather_wait(2, half(1, 0, 0))
    gather_send(16, block(1, 0), sibling)
    for c in range(4, ncol):
        transpose_w(c)
    gather_wait(6, half(2, 0, 0))
    gather_wait(7, half(2, 0, 1))
    gather_send(18, block(2, 0), sibling)
    transpose_cot()
    gather_wait(8, half(3, 1, 0))
    gather_send(12, half(3, 1, 0), right)
    gather_wait(11, half(1, 1, 1))
    gather_send(13, half(1, 1, 1), left)
    gather_wait(9, half(3, 1, 1))
    gather_send(19, block(3, 1), sibling)
    gather_wait(10, half(1, 1, 0))
    gather_send(20, block(1, 1), sibling)
    gather_wait(12, half(2, 1, 0))
    gather_wait(13, half(2, 1, 1))
    gather_send(21, block(2, 1), sibling)
    for m, (dx, dy) in zip(range(14, 22), ((0, 0), (3, 0), (1, 0), (0, 1), (2, 0), (3, 1), (1, 1), (2, 1))):
        gather_wait(m, block(dx, dy, 1))

    def column(c):
        for j in range(8):
            xs[c % 2, j * 128 : (j + 1) * 128, :] = xt[rows[(4 * ylo + j) % 8, s * ncol + c]]
        pre = dot_nn(wt[c], xs[c % 2])
        sig = jax.nn.sigmoid(pre)
        act[:, c * 128 : (c + 1) * 128] = (pre * sig).T.astype(BF16)
        slope = cott[c].astype(F32) * sig * (1.0 + pre * (1.0 - sig))
        dt[c * 128 : (c + 1) * 128, :] = slope.astype(BF16)
        grad = dot_nt(xs[c % 2], dt[c * 128 : (c + 1) * 128, :])
        own[c] = grad.reshape(2, NZ, 16, 128)
        if c < NB:
            ysend[c] = own[c, 1].astype(BF16)
            push(ysend.at[c], yrecv.at[c], y_s.at[c], y_r.at[c], dev_y)

    def holder(send, recv, s_sem, r_sem, part):
        def wait(d, e):
            remote(send.at[d, e], recv.at[d, e], s_sem.at[d, e], r_sem.at[d, e], sibling).wait_recv()
            return recv[d, e].astype(F32)

        def relay(*distances):
            for e in distances:
                for d in (0, 1):
                    if e >= top[d]:
                        continue
                    total = part((z + sign[d] * (e + 1) + NZ) % NZ)
                    for child in children(e, top[d]):
                        total = total + wait(d, child)
                    send[d, e] = total.astype(BF16)
                    push(send.at[d, e], recv.at[d, e], s_sem.at[d, e], r_sem.at[d, e], dev_z(sign[d] * hop(e)))

        def end():
            return part(z) + wait(0, 0) + wait(1, 0)

        return relay, end

    a_relay, a_end = holder(asend, arecv, a_s, a_r, lambda owner: own[NB:, :, owner])
    b_relay, b_end = holder(
        bsend, brecv, b_s, b_r, lambda owner: own[:NB, 0, owner] + yrecv[:, owner].astype(F32)
    )

    def partial(dx, dy, dc):
        weights = wd[pl.ds(2 * shard_at(dx, dy, dc), 2)].reshape(256, ncol * 128)
        return dot_nn(weights, dt[...])

    def sibling_task(p):
        dx, dy = others[p] if p < 7 else (0, 0)
        csend[p] = partial(dx, dy, 1).astype(BF16)
        push(csend.at[p], crecv.at[p], c_s.at[p], c_r.at[p], sibling)

    def chip_task(p):
        dx, dy = others[p] if p < 7 else (0, 0)
        total = partial(dx, dy, 0)
        remote(csend.at[p], crecv.at[p], c_s.at[p], c_r.at[p], sibling).wait_recv()
        total = total + crecv[p].astype(F32)
        if p == 7:
            gown[...] = total
            return
        gsend[p] = total.astype(BF16)
        push(gsend.at[p], grecv.at[p], g_s.at[p], g_r.at[p], dev_shard(dx, dy, 0))

    def gather_grad():
        total = gown[...]
        for p in range(7):
            remote(gsend.at[p], grecv.at[p], g_s.at[p], g_r.at[p], sibling).wait_recv()
            total = total + grecv[p].astype(F32)
        ig_out[...] = total.T.astype(BF16)

    for c in range(ncol):
        column(c)
    act_copy = pltpu.make_async_copy(act, act_out, act_sem)
    act_copy.start()
    a_relay(15, 13, 11, 7, 3)
    for c in range(ncol):
        dense_w(c)
    a_relay(14, 10, 6, 2)
    for p in range(0, 4):
        sibling_task(p)
    for c in range(NB):
        remote(ysend.at[c], yrecv.at[c], y_s.at[c], y_r.at[c], dev_y).wait_recv()
    b_relay(15, 13)
    a_relay(12, 9, 5)
    b_relay(11, 7, 3)
    for p in range(4, 8):
        sibling_task(p)
    b_relay(14, 10, 6, 2)
    a_relay(1)
    for p in range(0, 3):
        chip_task(p)
    a_relay(8)
    b_relay(12, 9, 5)
    for p in range(3, 8):
        chip_task(p)
    a_relay(4)
    b_relay(8, 1)
    gather_grad()
    a_relay(0)
    b_relay(4)
    scale = 1.0 / math.sqrt(tokens * lax.axis_size("replica"))
    last = a_end()
    fsend[...] = last[:, 1].astype(BF16)
    push(fsend, frecv, f_s, f_r, dev_y)
    b_relay(0)
    remote(fsend, frecv, f_s, f_r, dev_y).wait_recv()
    wg_out[NB:] = (last[:, 0] + frecv[...].astype(F32)) * scale
    wg_out[:NB] = b_end() * scale
    for copy in sends:
        copy.wait_send()
    act_copy.wait()


def place(a, b, c, a_out, b_out, c_out):
    a_out[...] = a[...]
    b_out[...] = b[...]
    c_out[...] = c[...]


def local(features, weight, rows_index, cotangent):
    tokens, width = features.shape
    columns, depth, side = weight.shape
    blocks = columns * depth // side
    dma = pltpu.SemaphoreType.DMA
    vmem = pl.BlockSpec(memory_space=pltpu.VMEM)
    anywhere = pl.BlockSpec(memory_space=pl.ANY)
    shapes = (
        jax.ShapeDtypeStruct((tokens, columns * side), BF16),
        jax.ShapeDtypeStruct((tokens, width), BF16),
        jax.ShapeDtypeStruct((columns, 16, side), F32),
    )
    results = pl.pallas_call(
        kernel,
        out_shape=shapes,
        in_specs=[pl.BlockSpec(memory_space=pltpu.SMEM), vmem, anywhere, anywhere],
        out_specs=(anywhere, vmem, vmem),
        scratch_shapes=[
            pltpu.VMEM((32, side, tokens), BF16),
            pltpu.VMEM((blocks + 1, side, side), BF16),
            pltpu.VMEM((columns, side, depth), BF16),
            pltpu.VMEM((32, side, columns * side), BF16),
            pltpu.VMEM((tokens, columns * side), BF16),
            pltpu.VMEM((columns, side, tokens), BF16),
            pltpu.VMEM((columns * side, tokens), BF16),
            pltpu.VMEM((2, depth, tokens), BF16),
            pltpu.VMEM((tokens, columns * side), BF16),
            pltpu.VMEM((columns, 2, NZ, 16, side), F32),
            pltpu.VMEM((2, NZ // 2, columns - NB, 2, 16, side), BF16),
            pltpu.VMEM((2, NZ // 2, columns - NB, 2, 16, side), BF16),
            pltpu.VMEM((2, NZ // 2, NB, 16, side), BF16),
            pltpu.VMEM((2, NZ // 2, NB, 16, side), BF16),
            pltpu.VMEM((NB, NZ, 16, side), BF16),
            pltpu.VMEM((NB, NZ, 16, side), BF16),
            pltpu.VMEM((columns - NB, 16, side), BF16),
            pltpu.VMEM((columns - NB, 16, side), BF16),
            pltpu.VMEM((8, 2 * side, tokens), BF16),
            pltpu.VMEM((8, 2 * side, tokens), BF16),
            pltpu.VMEM((7, 2 * side, tokens), BF16),
            pltpu.VMEM((7, 2 * side, tokens), BF16),
            pltpu.VMEM((2 * side, tokens), F32),
            dma((2,)), dma,
            dma((22,)), dma((22,)),
            dma((2, NZ // 2)), dma((2, NZ // 2)),
            dma((2, NZ // 2)), dma((2, NZ // 2)),
            dma((NB,)), dma((NB,)),
            dma, dma,
            dma((8,)), dma((8,)),
            dma((7,)), dma((7,)),
        ],
        compiler_params=pltpu.CompilerParams(
            collective_id=0, has_side_effects=True, vmem_limit_bytes=56 * 2**20
        ),
        name="fused",
    )(rows_index.T, features, weight.reshape(blocks, side, side), cotangent)
    return pl.pallas_call(
        place,
        out_shape=shapes,
        in_specs=[vmem] * 3,
        out_specs=(vmem,) * 3,
        name="place",
    )(*results)


def solution(mesh):
    placed = (P("replica", "shard"), P("shard", None, None), P(), P("replica", "shard"))
    return jax.shard_map(
        local,
        mesh=mesh,
        in_specs=placed,
        out_specs=(P("replica", "shard"), P("replica", "shard"), P("shard", "replica", None)),
        check_vma=False,
    )
```
